512 devices in a mesh: seq: 64 (over y, z_lo, core), strand: 2 (over z_hi), head: 4 (over x).
Axes of the slice: x: 4, y: 4, z: 16 (z_hi: 2, z_lo: 8; z = z_hi * 8 + z_lo), core: 2. Of those that a mesh axis runs over, the one named last changes fastest.
Arguments:
- top: bfloat16 [4, 2, 16384, 1536], P('head', 'strand', 'seq'), may hold values from -6 to 6
- grad_heads: bfloat16 [4, 2, 16384, 1536], P(None, 'strand', 'seq', 'head'), may hold values from -6 to 6
- tap_weight_grid: bfloat16 [3, 768, 768], P(None, 'seq'), may hold values from -0.125 to 0.125
- out_w: bfloat16 [768, 768], P('seq'), may hold values from -0.21875 to 0.21875
- mix_w: bfloat16 [768, 768], P('seq'), may hold values from -0.21875 to 0.21875
- rc_perm: int32 [768], replicated, may hold values from 0 to 767, each once
Outputs:
- restored: bfloat16 [4, 2, 16384, 1536], P('head', 'strand', 'seq')
- grad_input: bfloat16 [4, 2, 16384, 1536], P('head', 'strand', 'seq')
The draws below stay inside these ranges and needn't reach their ends.
Inputs may be any that keep to these rules, and one draw needn't show every extreme that they name: `rc_perm`: every channel index appears exactly once.
All inputs are finite; a program needn't handle non-finite values.
Results may differ from the reference program's by a relative error of at most 0.008.
Values may be sent and summed in bfloat16 or wider, within the bound.
No kernel may reach another device: no remote copies, remote signals or barrier semaphores. Data moves between devices by JAX's collectives and lax.ppermute only.
A program may use at most 64 MiB of HBM per device.

```python
import jax
import jax.numpy as jnp

C = 1536
HALF = 768
INNER = 768
DILATION_STEP = 128
SAMPLES = 4
POS = 16384


def block_scale(own_key, extent, cuts, smallest, top_value):
    level, own = 1.0, jax.random.fold_in(own_key, 6)
    for axis_at, blocks in cuts:
        heights = jnp.exp(jax.random.uniform(jax.random.fold_in(own, axis_at), (blocks,), jnp.float32, smallest / len(cuts), top_value / len(cuts)))
        level = level * jnp.repeat(heights, extent[axis_at] // blocks).reshape([-1 if axis == axis_at else 1 for axis in range(len(extent))])
    return level


def scatter_about(own_key, extent, deviation, most, pieces=(), kind=jnp.bfloat16):
    entries = jax.random.normal(own_key, extent, jnp.float32) * deviation
    if len(pieces) > 0:
        entries = block_scale(own_key, extent, pieces, -0.22, 0.18) * entries
    return jnp.clip(entries, min=-most, max=most).astype(kind)


def setup_inputs(seed: int = 0) -> dict:
    streams_of = jax.random.split(jax.random.key(seed), 7)
    return {
        "top": scatter_about(streams_of[0], (SAMPLES, 2, POS, C), 1.0, 6.0, ((0, 4), (1, 2), (2, 64))),
        "grad_heads": scatter_about(streams_of[1], (SAMPLES, 2, POS, C), 1.0, 6.0, ((1, 2), (2, 64), (3, 4))),
        "tap_weight_grid": scatter_about(streams_of[2], (3, HALF, INNER), (3 * HALF) ** -0.5, 0.125, ((1, 64),)),
        "out_w": scatter_about(streams_of[3], (INNER, HALF), INNER ** -0.5, 0.21875, ((0, 64),)),
        "mix_w": scatter_about(streams_of[4], (HALF, HALF), HALF ** -0.5, 0.21875, ((0, 64),)),
        "rc_perm": jax.random.permutation(streams_of[5], HALF).astype(jnp.int32),
    }


def product(left, right):
    return jnp.einsum('spc,cd->spd', left.astype(jnp.float32), right.astype(jnp.float32))

def dilated_result(field, kernel, dilation):
    length = field.shape[1]
    padded = jnp.pad(field, ((0, 0), (dilation, dilation), (0, 0)))
    total = jnp.zeros((field.shape[0], length, kernel.shape[2]), jnp.float32)
    for offset in range(3):
        window = padded[:, offset * dilation:offset * dilation + length]
        total = total + product(window, kernel[offset])
    return total

def transposed_result(grad, kernel, dilation):
    length = grad.shape[1]
    padded = jnp.pad(grad, ((0, 0), (dilation, dilation), (0, 0)))
    total = jnp.zeros((grad.shape[0], length, kernel.shape[1]), jnp.float32)
    for offset in range(3):
        start = (2 - offset) * dilation
        window = padded[:, start:start + length]
        total = total + product(window, kernel[offset].T)
    return total

def one_sample(top, grads, tap_weight_grid, out_w, mix_w, rc_perm, inverse):
    top_a = top[..., :HALF]
    top_b = top[..., HALF:]
    mirror = jnp.take(top_a[::-1], rc_perm, axis=2)
    paired = (top_a.astype(jnp.float32) + mirror.astype(jnp.float32)).astype(jnp.bfloat16)
    second_input = (top_b.astype(jnp.float32) - product(paired, mix_w)).astype(jnp.bfloat16)
    preactivation_rows = dilated_result(second_input, tap_weight_grid, DILATION_STEP)
    hidden = jax.nn.gelu(preactivation_rows).astype(jnp.bfloat16)
    input_a = (top_a.astype(jnp.float32) - product(hidden, out_w)).astype(jnp.bfloat16)
    grad_a = grads[..., :HALF]
    second_gradient = grads[..., HALF:]
    backed = product(second_gradient, mix_w.T).astype(jnp.bfloat16)
    returned = jnp.take(backed, inverse, axis=2)[::-1]
    cot_a = (grad_a.astype(jnp.float32) + backed.astype(jnp.float32) + returned.astype(jnp.float32)).astype(jnp.bfloat16)
    pulled = product(cot_a, out_w.T)
    unused, slope = jax.vjp(jax.nn.gelu, preactivation_rows)
    preactivation_cotangent = slope(pulled)[0].astype(jnp.bfloat16)
    cotangent_second = (second_gradient.astype(jnp.float32) + transposed_result(preactivation_cotangent, tap_weight_grid, DILATION_STEP)).astype(jnp.bfloat16)
    return (jnp.concatenate([input_a, second_input], axis=2), jnp.concatenate([cot_a, cotangent_second], axis=2))

def reference(top, grad_heads, tap_weight_grid, out_w, mix_w, rc_perm):
    inverse = jnp.zeros((HALF,), jnp.int32).at[rc_perm].set(jnp.arange(HALF, dtype=jnp.int32))
    restored_list = []
    grad_list = []
    for sample in range(SAMPLES):
        restored_one, grad_one = one_sample(top[sample], grad_heads[sample], tap_weight_grid, out_w, mix_w, rc_perm, inverse)
        restored_list.append(restored_one)
        grad_list.append(grad_one)
    return (jnp.stack(restored_list), jnp.stack(grad_list))
```

```python
import jax
import jax.numpy as jnp
from jax import lax
from jax.experimental import pallas as pl
from jax.experimental.pallas import tpu as pltpu
from jax.sharding import PartitionSpec as P

BF16, F32 = jnp.bfloat16, jnp.float32
SHARE = 2


def pairwise(value, bit):
    count = lax.axis_size("seq")
    if bit == 0:
        pairs = [(i, i ^ 1) for i in range(count)]
    else:
        pairs = [(i, i + 1) for i in range(1, count - 1, 2)] + [(i + 1, i) for i in range(1, count - 1, 2)]
    return lax.ppermute(value, "seq", pairs)


def mirrored(value):
    return lax.ppermute(value, "strand", [(0, 1), (1, 0)])


def spread(piece, axes, groups):
    count = len(groups[0])
    sent = jnp.broadcast_to(piece[None], (count, *piece.shape))
    return lax.all_to_all(sent, axes, 0, 0, axis_index_groups=groups, tiled=True)


def piece_of(tap_weight_grid, out_w, mix_w, core):
    heads = lax.axis_size("head")
    own = jnp.concatenate([tap_weight_grid, out_w[None], mix_w[None]], axis=0)
    other = pairwise(own, 0)
    low = jnp.where(core == 0, own, other)
    high = jnp.where(core == 0, other, own)
    mats, rows, width = own.shape
    slabs = jnp.concatenate([low, high], axis=1).reshape(mats * 2 * rows // 8, 8, width)
    slabs = jnp.pad(slabs, ((0, 2 * heads * SHARE - slabs.shape[0]), (0, 0), (0, 0)))
    return lax.dynamic_slice_in_dim(slabs, (2 * lax.axis_index("head") + core) * SHARE, SHARE, 0)


def assemble_kernel(core_ref, own_ref, other_ref, mats_ref, sems):
    core = core_ref[0]
    thirds = mats_ref.shape[2]

    def copies(flag):
        made = []
        for k in range(mats_ref.shape[0] * thirds):
            mat, third = k // thirds, k % thirds
            head, side, slot = k // (2 * SHARE), k // SHARE % 2, k % SHARE
            source = own_ref if side == flag else other_ref
            place = (2 - mat if flag and mat < 3 else mat)
            made.append(
                pltpu.make_async_copy(source.at[head, :, slot], mats_ref.at[place, :, third], sems.at[k])
            )
        return made

    for flag in range(2):

        @pl.when(core == flag)
        def _():
            made = copies(flag)
            for copy in made:
                copy.start()
            for copy in made:
                copy.wait()


def assembled(own, other, core, mats):
    _, blocks, _, eight, width = own.shape
    thirds = width // (blocks * eight)
    out = pl.pallas_call(
        assemble_kernel,
        out_shape=jax.ShapeDtypeStruct((mats, blocks, thirds, eight, width), own.dtype),
        in_specs=[
            pl.BlockSpec(memory_space=pltpu.SMEM),
            pl.BlockSpec(memory_space=pl.ANY),
            pl.BlockSpec(memory_space=pl.ANY),
        ],
        out_specs=pl.BlockSpec(memory_space=pltpu.VMEM),
        scratch_shapes=[pltpu.SemaphoreType.DMA((mats * thirds,))],
        cost_estimate=pl.CostEstimate(flops=0, bytes_accessed=4 * own.size * 2, transcendentals=0),
        name="assemble",
    )(core[None], own, other)
    return out.reshape(mats, blocks * thirds * eight, width)


def dot(a, b):
    return jnp.dot(a, b, preferred_element_type=F32)


def dot_t(a, b):
    return jnp.einsum("pd,cd->pc", a, b, preferred_element_type=F32)


def shards(top, grad_heads, tap_weight_grid, out_w, mix_w, rc_perm):
    half = top.shape[3] // 2
    rows = top.shape[2] // 2
    ranks, heads = 4, lax.axis_size("head")
    lines = lax.axis_size("seq") // (2 * ranks)
    core = lax.axis_index("seq") % 2
    outer, inner = core * rows, (1 - core) * rows

    def cut(array, start):
        return lax.dynamic_slice_in_dim(array, start, rows, 0)

    top = top[0, 0]
    a_out, b_out = cut(top, outer)[:, :half], cut(top, outer)[:, half:]
    a_in, b_in = cut(top, inner)[:, :half], cut(top, inner)[:, half:]
    ao_out = mirrored(a_out)
    ao_in = mirrored(a_in)
    cotan = lax.all_to_all(grad_heads, "head", split_axis=0, concat_axis=0, tiled=True)[:, 0]
    cotan = cotan.transpose(1, 0, 2).reshape(2 * rows, 2 * half)
    ga_out, gb_out = cut(cotan, outer)[:, :half], cut(cotan, outer)[:, half:]
    ga_in, gb_in = cut(cotan, inner)[:, :half], cut(cotan, inner)[:, half:]
    go_out = mirrored(gb_out)
    go_in = mirrored(gb_in)

    piece = piece_of(tap_weight_grid, out_w, mix_w, core)
    along = [[(y * lines + z) * 2 + c for z in range(lines)] for y in range(ranks) for c in range(2)]
    line = spread(piece, "seq", along)
    plane = [
        [h * 2 * lines * ranks + (y * lines + z) * 2 + c for h in range(heads) for y in range(ranks)]
        for z in range(lines)
        for c in range(2)
    ]
    part = spread(line, ("head", "seq"), plane)
    part = part.reshape(heads, ranks * lines, *part.shape[2:])
    partner = pairwise(part, 0)
    mats = assembled(part, partner, core, 5)
    first, middle, last, out_full, mix_full = (mats[k] for k in range(5))
    onehot = (lax.broadcasted_iota(jnp.int32, (half, half), 0) == rc_perm[None, :]).astype(BF16)
    turned = dot(onehot, mix_full).astype(BF16)

    def restore_b(b, a, ao):
        return (b.astype(F32) - (dot(a, mix_full) + dot(ao, turned))).astype(BF16)

    sb_out = restore_b(b_out, a_out, ao_out)
    ext = pairwise(sb_out, 1)
    sb_in = restore_b(b_in, a_in, ao_in)
    across = pairwise(sb_in, 0)
    pre_out = dot(ext, first) + dot(sb_out, middle) + dot(sb_in, last)
    pre_in = dot(sb_out, first) + dot(sb_in, middle) + dot(across, last)

    def branch(pre, a):
        value, slope = jax.vjp(jax.nn.gelu, pre)
        ia = (a.astype(F32) - dot(value.astype(BF16), out_full)).astype(BF16)
        return ia, slope(jnp.ones_like(pre))[0]

    ia_out, slope_out = branch(pre_out, a_out)
    ia_in, slope_in = branch(pre_in, a_in)

    def pull(ga, gb, go, slope):
        cot = (ga.astype(F32) + dot_t(gb, mix_full) + dot_t(go, turned)).astype(BF16)
        return cot, (dot_t(cot, out_full) * slope).astype(BF16)

    ca_out, cp_out = pull(ga_out, gb_out, go_out, slope_out)
    cext = pairwise(cp_out, 1)
    ca_in, cp_in = pull(ga_in, gb_in, go_in, slope_in)
    cacross = pairwise(cp_in, 0)
    cb_out = (
        gb_out.astype(F32) + dot_t(cp_in, first) + dot_t(cp_out, middle) + dot_t(cext, last)
    ).astype(BF16)
    cb_in = (
        gb_in.astype(F32) + dot_t(cacross, first) + dot_t(cp_in, middle) + dot_t(cp_out, last)
    ).astype(BF16)

    def placed(a_o, b_o, a_i, b_i):
        o, i = jnp.concatenate([a_o, b_o], 1), jnp.concatenate([a_i, b_i], 1)
        return jnp.where(core == 0, jnp.concatenate([o, i], 0), jnp.concatenate([i, o], 0))[None, None]

    return placed(ia_out, sb_out, ia_in, sb_in), placed(ca_out, cb_out, ca_in, cb_in)


def solution(mesh):
    placed = (
        P("head", "strand", "seq", None),
        P(None, "strand", "seq", "head"),
        P(None, "seq", None),
        P("seq", None),
        P("seq", None),
        P(),
    )
    return jax.shard_map(
        shards,
        mesh=mesh,
        in_specs=placed,
        out_specs=(P("head", "strand", "seq", None), P("head", "strand", "seq", None)),
        check_vma=False,
    )
```

```python
import functools

import jax
import jax.numpy as jnp
from jax import lax
from jax.experimental import pallas as pl
from jax.experimental.pallas import tpu as pltpu
from jax.sharding import PartitionSpec as P

BF16, F32 = jnp.bfloat16, jnp.float32
LANES = 128


def pairwise(value, bit):
    count = lax.axis_size("seq")
    if bit == 0:
        pairs = [(i, i ^ 1) for i in range(count)]
    else:
        pairs = [(i, i + 1) for i in range(1, count - 1, 2)] + [(i + 1, i) for i in range(1, count - 1, 2)]
    return lax.ppermute(value, "seq", pairs)


def mirrored(value):
    return lax.ppermute(value, "strand", [(0, 1), (1, 0)])


def dot(a, b):
    return lax.dot_general(a, b, (((1,), (0,)), ((), ())), preferred_element_type=F32)


def dot_t(a, b):
    return lax.dot_general(a, b, (((1,), (1,)), ((), ())), preferred_element_type=F32)


def at(start, size):
    return pl.ds(pl.multiple_of(start, LANES), size)


def call(kernel, place, ins, outs, flops, scratch=(), limit=24):
    moved = sum(a.size * a.dtype.itemsize for a in ins) + sum(
        o.size * jnp.dtype(o.dtype).itemsize for o in outs
    )
    return pl.pallas_call(
        kernel,
        out_shape=outs,
        in_specs=[pl.BlockSpec(memory_space=pltpu.SMEM)]
        + [pl.BlockSpec(memory_space=pltpu.VMEM)] * len(ins),
        out_specs=[pl.BlockSpec(memory_space=pltpu.VMEM)] * len(outs),
        scratch_shapes=list(scratch),
        compiler_params=pltpu.CompilerParams(vmem_limit_bytes=limit << 20),
        cost_estimate=pl.CostEstimate(flops=flops, bytes_accessed=moved, transcendentals=0),
    )(place, *ins)


def shape(dims, kind):
    return jax.ShapeDtypeStruct(dims, kind)


def split(place, taps, out, mix, sent):
    head = place[1]
    wide = sent.shape[3] - LANES
    carried = jnp.where(head == 3, out[...], taps[jnp.minimum(head, 2)])
    for c in range(2):
        column = (2 * jnp.minimum(head, 2) + c) * LANES
        sent[0, c, :, :wide] = carried[:, c * wide : (c + 1) * wide]
        sent[0, c, :, wide:] = mix[:, at(column, LANES)]
    for k in range(1, sent.shape[0]):
        sent[k] = sent[0]


def repack(place, line, sent):
    deep = line.shape[1]
    for z in range(sent.shape[1]):
        sent[0, z, :deep, :] = line[2 * z]
        sent[0, z, deep:, :] = line[2 * z + 1]
    for k in range(1, sent.shape[0]):
        sent[k] = sent[0]


def turn(core, perm, grads, own, other, mix, turned, base):
    c = core[0]
    side = mix.shape[0]
    wide = grads.shape[2]
    hot = (lax.broadcasted_iota(jnp.int32, (side, side), 0) == perm[...]).astype(BF16)
    for k in range(side // (2 * LANES)):
        for place, source in ((c, own), (1 - c, other)):
            column = at((2 * k + place) * LANES, LANES)
            block = source[k, :, wide:]
            mix[:, column] = block
            turned[:, column] = dot(hot, block).astype(BF16)
    head = core[1]
    backed = dot_t(grads[head ^ 2], mix[:, :wide]) + dot_t(grads[head ^ 3], mix[:, wide:])
    for k in range(2):
        lane = slice(k * wide, (k + 1) * wide)
        base[:, lane] = grads[head ^ k].astype(F32) + backed[:, lane]


def restore(core, top, mirror, mix, turned, edge, inner):
    c = core[0]
    rows, half = edge.shape
    for result, place in ((edge, c), (inner, 1 - c)):
        line = at(place * rows, rows)
        mixing = dot(top[line, :half], mix[...]) + dot(mirror[line, :], turned[...])
        result[...] = (top[line, half:].astype(F32) - mixing).astype(BF16)


def branch(core, top, beyond, edge, inner, across, own, other, restored, slope, out, near):
    c = core[0]
    rows, half = edge.shape
    before = jnp.concatenate([beyond[...], edge[...]], axis=0)
    here = jnp.concatenate([edge[...], inner[...]], axis=0)
    after = jnp.concatenate([inner[...], across[...]], axis=0)
    wide = half // 2
    lines = (at(c * rows, rows), at((1 - c) * rows, rows))
    hidden = []
    root = 0.7978845608028654
    for place, taps in ((c, own), (1 - c, other)):
        lane = at(place * wide, wide)
        pre = dot(before, taps[2 * c, :, :wide]) + dot(here, taps[1, :, :wide]) + dot(after, taps[2 - 2 * c, :, :wide])
        squared = pre * pre
        bent = jnp.tanh(root * (pre + 0.044715 * (pre * squared)))
        share = 0.5 * (1.0 + bent)
        gain = share + pre * (0.5 * (1.0 - bent * bent)) * (root * (1.0 + 3.0 * 0.044715 * squared))
        hidden.append((pre * share).astype(BF16))
        for k in range(2):
            slope[k, :, lane] = gain[k * rows : (k + 1) * rows]
        out[:, lane] = taps[3, :, :wide]
        near[:, lane] = taps[2 * c, :, :wide]
    for place in (c, 1 - c):
        lane = at(place * wide, wide)
        made = dot(hidden[0], out[at(c * wide, wide), lane]) + dot(
            hidden[1], out[at((1 - c) * wide, wide), lane]
        )
        for k, line in enumerate(lines):
            restored[line, lane] = (
                top[line, lane].astype(F32) - made[k * rows : (k + 1) * rows]
            ).astype(BF16)
    restored[lines[0], half:] = edge[...]
    restored[lines[1], half:] = inner[...]


def pull(which, core, mirror, turned, base, slope, out, cot, held):
    c = core[0]
    rows = cot.shape[0]
    line = at((c if which == 0 else 1 - c) * rows, rows)
    wide = mirror.shape[2]
    odd = core[1] & 1
    total = base[line, :]
    for k in range(mirror.shape[0]):
        total += dot_t(mirror[k ^ odd], turned[:, k * wide : (k + 1) * wide])
    rounded = total.astype(BF16)
    cot[...] = rounded
    held[...] = (dot_t(rounded, out[...]) * slope[which]).astype(BF16)


def gather(core, grads, beyond, edge, inner, own, other, result, rest):
    c = core[0]
    rows, half = edge.shape
    wide = half // 2
    head = core[1]
    total = jnp.zeros((2 * rows, half), F32)
    low = jnp.zeros((rows, half), F32)
    for place, taps in ((c, own), (1 - c, other)):
        lane = at(place * wide, wide)
        e, i = edge[:, lane], inner[:, lane]
        total += dot_t(jnp.concatenate([e, i], axis=0), taps[1, :, :wide])
        total += dot_t(jnp.concatenate([beyond[:, lane], e], axis=0), taps[2 - 2 * c, :, :wide])
        low += dot_t(i, taps[2 * c, :, :wide])
    lines = (at(c * rows, rows), at((1 - c) * rows, rows))
    plain = [
        jnp.concatenate([grads[head ^ 2, line, :], grads[head ^ 3, line, :]], axis=1).astype(F32)
        for line in lines
    ]
    result[...] = (plain[0] + total[:rows] + low).astype(BF16)
    rest[...] = plain[1] + total[rows:]


def finish(core, across, near, edge_a, inner_a, edge_b, rest, result):
    c = core[0]
    rows, half = edge_a.shape
    first, second = at(c * rows, rows), at((1 - c) * rows, rows)
    result[first, :half] = edge_a[...]
    result[second, :half] = inner_a[...]
    result[first, half:] = edge_b[...]
    result[second, half:] = (rest[...] + dot_t(across[...], near[...])).astype(BF16)


def shards(top, grad_heads, tap_weight_grid, out_w, mix_w, rc_perm):
    half = top.shape[3] // 2
    rows = top.shape[2] // 2
    heads = lax.axis_size("head")
    ranks = 4
    lines = lax.axis_size("seq") // (2 * ranks)
    core = lax.axis_index("seq") % 2
    head = lax.axis_index("head")
    top = top[0, 0]

    place = jnp.stack([core, head]).astype(jnp.int32)
    deep = out_w.shape[0]
    (sent,) = call(
        split,
        place,
        (tap_weight_grid, out_w, mix_w),
        (shape((lines, 2, deep, half // 2 + LANES), BF16),),
        0,
    )
    along = [[(y * lines + z) * 2 + c for z in range(lines) for c in range(2)] for y in range(ranks)]
    line = lax.all_to_all(sent.reshape(2 * lines, *sent.shape[2:]), "seq", 0, 0, axis_index_groups=along, tiled=True)
    ao = mirrored(top[:, :half])
    blocks = [lax.dynamic_index_in_dim(grad_heads[:, 0], head ^ k, 0, False) for k in range(heads)]
    grads = [blocks[0]]
    for k in range(1, heads):
        grads.append(lax.ppermute(blocks[k], "head", [(i, i ^ k) for i in range(heads)]))
    grads = jnp.stack(grads)

    def sent_chunk(start):
        return lax.dynamic_slice(grads, (2 - (head // 2) * 2, start, 0), (2, rows, grads.shape[2]))

    go_edge = mirrored(sent_chunk(core * rows))
    go_inner = mirrored(sent_chunk((1 - core) * rows))
    plane = [
        [h * 2 * lines * ranks + (y * lines + z) * 2 + c for h in range(heads) for y in range(ranks)]
        for z in range(lines)
        for c in range(2)
    ]
    (sent,) = call(
        repack, place, (line,), (shape((heads * ranks, lines, 2 * deep, line.shape[2]), BF16),), 0
    )
    mine = lax.all_to_all(sent, ("head", "seq"), 0, 0, axis_index_groups=plane, tiled=True)
    mine = mine.reshape(heads, half, mine.shape[3])
    theirs = pairwise(mine, 0)

    unit = 2 * rows * half * half
    square, tall, chunk = (half, half), (2 * rows, half), (rows, half)
    mix, turned, base = call(
        turn,
        place,
        (rc_perm[None, :], grads, mine, theirs),
        (shape(square, BF16), shape(square, BF16), shape(tall, F32)),
        8 * unit,
    )
    edge, inner = call(
        restore, place, (top, ao, mix, turned), (shape(chunk, BF16), shape(chunk, BF16)), 4 * unit
    )
    beyond = pairwise(edge, 1)
    across = pairwise(inner, 0)
    restored, slope, out, near = call(
        branch,
        place,
        (top, beyond, edge, inner, across, mine, theirs),
        (shape(top.shape, BF16), shape((2, *chunk), F32), shape(square, BF16), shape(square, BF16)),
        8 * unit,
        limit=32,
    )
    pulls = []
    for which, mirror in ((0, go_edge), (1, go_inner)):
        cot, held = call(
            functools.partial(pull, which),
            place,
            (mirror, turned, base, slope, out),
            (shape(chunk, BF16), shape(chunk, BF16)),
            2 * unit,
        )
        pulls.append((cot, held))
    cot_beyond = pairwise(pulls[0][1], 1)
    cot_across = pairwise(pulls[1][1], 0)
    edge_b, rest = call(
        gather,
        place,
        (grads, cot_beyond, pulls[0][1], pulls[1][1], mine, theirs),
        (shape(chunk, BF16), shape(chunk, F32)),
        5 * unit,
        limit=32,
    )
    (result,) = call(
        finish,
        place,
        (cot_across, near, pulls[0][0], pulls[1][0], edge_b, rest),
        (shape(top.shape, BF16),),
        unit,
    )
    return restored[None, None], result[None, None]


def solution(mesh):
    placed = (
        P("head", "strand", "seq", None),
        P(None, "strand", "seq", "head"),
        P(None, "seq", None),
        P("seq", None),
        P("seq", None),
        P(),
    )
    return jax.shard_map(
        shards,
        mesh=mesh,
        in_specs=placed,
        out_specs=(P("head", "strand", "seq", None), P("head", "strand", "seq", None)),
        check_vma=False,
    )
```

```python
import jax
import jax.numpy as jnp
from jax import lax
from jax.experimental import pallas as pl
from jax.experimental.pallas import tpu as pltpu
from jax.sharding import PartitionSpec as P

BF16, F32 = jnp.bfloat16, jnp.float32
LANES = 128


def pairwise(value, bit):
    count = lax.axis_size("seq")
    if bit == 0:
        pairs = [(i, i ^ 1) for i in range(count)]
    else:
        pairs = [(i, i + 1) for i in range(1, count - 1, 2)] + [(i + 1, i) for i in range(1, count - 1, 2)]
    return lax.ppermute(value, "seq", pairs)


def mirrored(value):
    return lax.ppermute(value, "strand", [(0, 1), (1, 0)])


def dot(a, b):
    return lax.dot_general(a, b, (((1,), (0,)), ((), ())), preferred_element_type=F32)


def dot_t(a, b):
    return lax.dot_general(a, b, (((1,), (1,)), ((), ())), preferred_element_type=F32)


def at(start, size):
    return pl.ds(pl.multiple_of(start, LANES), size)


def call(kernel, ins, outs, flops, scratch=(), limit=24, space=pltpu.VMEM):
    moved = sum(a.size * a.dtype.itemsize for a in ins) + sum(
        o.size * jnp.dtype(o.dtype).itemsize for o in outs
    )

    def body(*refs):
        kernel((lax.rem(lax.axis_index("seq"), 2), lax.axis_index("head")), *refs)

    return pl.pallas_call(
        body,
        out_shape=outs,
        in_specs=[pl.BlockSpec(memory_space=pltpu.VMEM)] * len(ins),
        out_specs=[pl.BlockSpec(memory_space=space)] * len(outs),
        scratch_shapes=list(scratch),
        compiler_params=pltpu.CompilerParams(vmem_limit_bytes=limit << 20),
        cost_estimate=pl.CostEstimate(flops=flops, bytes_accessed=moved, transcendentals=0),
    )(*ins)


def shape(dims, kind):
    return jax.ShapeDtypeStruct(dims, kind)


def split(place, taps, out, mix, sent):
    head = place[1]
    wide = sent.shape[3] - LANES
    carried = jnp.where(head == 3, out[...], taps[jnp.minimum(head, 2)])
    for c in range(2):
        column = (2 * jnp.minimum(head, 2) + c) * LANES
        sent[0, c, :, :wide] = carried[:, c * wide : (c + 1) * wide]
        sent[0, c, :, wide:] = mix[:, at(column, LANES)]
    for k in range(1, sent.shape[0]):
        sent[k] = sent[0]


def repack(place, line, sent):
    deep = line.shape[1]
    for z in range(sent.shape[1]):
        sent[0, z, :deep, :] = line[2 * z]
        sent[0, z, deep:, :] = line[2 * z + 1]
    for k in range(1, sent.shape[0]):
        sent[k] = sent[0]


def mirror_sum(core, perm, top, mirror, both):
    half = both.shape[2]
    hot = (lax.broadcasted_iota(jnp.int32, (half, half), 0) == perm[...]).astype(BF16)
    both[0] = (top[:, :half].astype(F32) + dot(mirror[...], hot)).astype(BF16)
    both[1] = top[:, half:]


def restore(core, paired, own, other, edge, inner):
    c = core[0]
    rows, half = edge.shape
    for k in range(half // (2 * LANES)):
        for place, pieces in ((c, own), (1 - c, other)):
            column = (2 * k + place) * LANES
            mixing = dot(paired[0], pieces[k])
            b = (paired[1, :, at(column, LANES)].astype(F32) - mixing).astype(BF16)

            @pl.when(c == 0)
            def _():
                edge[:, at(column, LANES)] = b[:rows]
                inner[:, at(column, LANES)] = b[rows:]

            @pl.when(c == 1)
            def _():
                edge[:, at(column, LANES)] = b[rows:]
                inner[:, at(column, LANES)] = b[:rows]


def turn(core, perm, grads, own, other, turned, base, mix):
    c, head = core[0], core[1]
    side = turned.shape[0]
    wide = side // 2
    hot = (lax.broadcasted_iota(jnp.int32, (side, side), 0) == perm[...]).astype(BF16)
    for place, pieces in ((c, own), (1 - c, other)):
        for k in range(side // (2 * LANES)):
            row = at((2 * k + place) * LANES, LANES)
            block = pieces[k]
            mix[row, :] = block.T
            turned[row, :] = dot(hot, block).astype(BF16).T
    backed = dot(grads[head ^ 2], mix[:wide, :]) + dot(grads[head ^ 3], mix[wide:, :])
    for k in range(2):
        lane = slice(k * wide, (k + 1) * wide)
        base[:, lane] = grads[head ^ k].astype(F32) + backed[:, lane]


def branch(core, beyond, edge, inner, across, own, other, hidden, slope, out):
    c = core[0]
    _, half = edge.shape
    before = jnp.concatenate([beyond[...], edge[...]], axis=0)
    here = jnp.concatenate([edge[...], inner[...]], axis=0)
    after = jnp.concatenate([inner[...], across[...]], axis=0)
    wide = half // 2
    root = 0.7978845608028654
    for place, taps in ((c, own), (1 - c, other)):
        lane = at(place * wide, wide)
        pre = (
            dot(before, taps[2 * c, :, :wide])
            + dot(here, taps[1, :, :wide])
            + dot(after, taps[2 - 2 * c, :, :wide])
        )
        squared = pre * pre
        bent = jnp.tanh(root * (pre + 0.044715 * (pre * squared)))
        share = 0.5 * (1.0 + bent)
        slope[:, lane] = share + pre * (0.5 * (1.0 - bent * bent)) * (
            root * (1.0 + 3.0 * 0.044715 * squared)
        )
        hidden[:, lane] = (pre * share).astype(BF16)
        out[lane, :] = taps[3, :, :wide].T


def emit(core, top, hidden, edge, inner, own, other, after, restored):
    c = core[0]
    rows, half = edge.shape
    wide = half // 2
    lines = (at(c * rows, rows), at((1 - c) * rows, rows))
    for place, pieces in ((c, own), (1 - c, other)):
        lane = at(place * wide, wide)
        made = dot(hidden[...], pieces[3, :, :wide])
        for k, line in enumerate(lines):
            restored[line, lane] = (
                top[line, lane].astype(F32) - made[k * rows : (k + 1) * rows]
            ).astype(BF16)
    restored[lines[0], half:] = edge[...]
    restored[lines[1], half:] = inner[...]


def pull(core, mirror, turned, base, slope, out, cot, edge, inner):
    c = core[0]
    rows = edge.shape[0]
    wide = mirror.shape[2]
    odd = core[1] & 1
    rounded = (
        base[...] + dot(mirror[odd], turned[:wide, :]) + dot(mirror[1 - odd], turned[wide:, :])
    ).astype(BF16)
    cot[...] = rounded
    pulled = dot(rounded, out[...])

    @pl.when(c == 0)
    def _():
        edge[...] = (pulled[:rows] * slope[:rows, :]).astype(BF16)
        inner[...] = (pulled[rows:] * slope[rows:, :]).astype(BF16)

    @pl.when(c == 1)
    def _():
        edge[...] = (pulled[rows:] * slope[:rows, :]).astype(BF16)
        inner[...] = (pulled[:rows] * slope[rows:, :]).astype(BF16)


def gather(core, grads, beyond, edge, inner, own, other, result, rest, near):
    c = core[0]
    rows, half = edge.shape
    wide = half // 2
    head = core[1]
    total = jnp.zeros((2 * rows, half), F32)
    low = jnp.zeros((rows, half), F32)
    for place, taps in ((c, own), (1 - c, other)):
        lane = at(place * wide, wide)
        e, i = edge[:, lane], inner[:, lane]
        total += dot_t(jnp.concatenate([e, i], axis=0), taps[1, :, :wide])
        total += dot_t(jnp.concatenate([beyond[:, lane], e], axis=0), taps[2 - 2 * c, :, :wide])
        low += dot_t(i, taps[2 * c, :, :wide])
        near[lane, :] = taps[2 * c, :, :wide].T
    lines = (at(c * rows, rows), at((1 - c) * rows, rows))
    plain = [
        jnp.concatenate([grads[head ^ 2, line, :], grads[head ^ 3, line, :]], axis=1).astype(F32)
        for line in lines
    ]
    result[...] = (plain[0] + total[:rows] + low).astype(BF16)
    rest[...] = plain[1] + total[rows:]


def finish(core, across, near, cot, edge_b, rest, result):
    c = core[0]
    rows = edge_b.shape[0]
    half = cot.shape[1]
    result[:, :half] = cot[...]
    result[at(c * rows, rows), half:] = edge_b[...]
    result[at((1 - c) * rows, rows), half:] = (rest[...] + dot(across[...], near[...])).astype(BF16)


def shards(top, grad_heads, tap_weight_grid, out_w, mix_w, rc_perm):
    half = top.shape[3] // 2
    rows = top.shape[2] // 2
    heads = lax.axis_size("head")
    ranks = 4
    lines = lax.axis_size("seq") // (2 * ranks)
    head = lax.axis_index("head")
    top = top[0, 0]

    deep = out_w.shape[0]
    (sent,) = call(
        split,
        (tap_weight_grid, out_w, mix_w),
        (shape((lines, 2, deep, half // 2 + LANES), BF16),),
        0,
        limit=60,
    )
    along = [[(y * lines + z) * 2 + c for z in range(lines) for c in range(2)] for y in range(ranks)]
    line = lax.all_to_all(
        sent.reshape(2 * lines, *sent.shape[2:]), "seq", 0, 0, axis_index_groups=along, tiled=True
    )
    ao = mirrored(top[:, :half])
    blocks = [lax.dynamic_index_in_dim(grad_heads[:, 0], head ^ k, 0, False) for k in range(heads)]
    grads = [blocks[0]]
    for k in range(1, heads):
        grads.append(lax.ppermute(blocks[k], "head", [(i, i ^ k) for i in range(heads)]))
    grads = jnp.stack(grads)

    go = mirrored(lax.dynamic_slice_in_dim(grads, 2 - (head // 2) * 2, 2, 0))
    plane = [
        [h * 2 * lines * ranks + (y * lines + z) * 2 + c for h in range(heads) for y in range(ranks)]
        for z in range(lines)
        for c in range(2)
    ]

    width = line.shape[2]
    (sent,) = call(repack, (line,), (shape((heads * ranks, lines, 2 * deep, width), BF16),), 0)
    both = lax.all_to_all(sent, ("head", "seq"), 0, 0, axis_index_groups=plane, tiled=True)
    both = both.reshape(heads, half, width)
    mine_mix = both[: half // (2 * LANES), :, half // 2 :]
    theirs_mix = pairwise(mine_mix, 0)
    mine = both
    theirs = pairwise(both, 0)

    unit = 2 * rows * half * half
    square, tall, chunk = (half, half), (2 * rows, half), (rows, half)
    perm = rc_perm[None, :]
    (paired,) = call(mirror_sum, (perm, top, ao), (shape((2, *tall), BF16),), 2 * unit)
    edge, inner = call(
        restore, (paired, mine_mix, theirs_mix), (shape(chunk, BF16), shape(chunk, BF16)), 2 * unit
    )
    beyond = pairwise(edge, 1)
    across = pairwise(inner, 0)
    turned, base = call(
        turn,
        (perm, grads, mine_mix, theirs_mix),
        (shape(square, BF16), shape(tall, F32)),
        6 * unit,
        scratch=(pltpu.VMEM(square, BF16),),
    )
    hidden, slope, out = call(
        branch,
        (beyond, edge, inner, across, mine, theirs),
        (shape(tall, BF16), shape(tall, F32), shape(square, BF16)),
        6 * unit,
    )
    cot, held_edge, held_inner = call(
        pull,
        (go, turned, base, slope, out),
        (shape(tall, BF16), shape(chunk, BF16), shape(chunk, BF16)),
        4 * unit,
    )
    cot_beyond = pairwise(held_edge, 1)
    cot_across = pairwise(held_inner, 0)
    (restored,) = call(
        emit,
        (top, hidden, edge, inner, mine, theirs, held_inner),
        (shape(top.shape, BF16),),
        2 * unit,
    )
    edge_b, rest, near = call(
        gather,
        (grads, cot_beyond, held_edge, held_inner, mine, theirs),
        (shape(chunk, BF16), shape(chunk, F32), shape(square, BF16)),
        5 * unit,
    )
    (result,) = call(
        finish,
        (cot_across, near, cot, edge_b, rest),
        (shape(top.shape, BF16),),
        unit,
    )
    return restored[None, None], result[None, None]


def solution(mesh):
    placed = (
        P("head", "strand", "seq", None),
        P(None, "strand", "seq", "head"),
        P(None, "seq", None),
        P("seq", None),
        P("seq", None),
        P(),
    )
    return jax.shard_map(
        shards,
        mesh=mesh,
        in_specs=placed,
        out_specs=(P("head", "strand", "seq", None), P("head", "strand", "seq", None)),
        check_vma=False,
    )
```

```python
import functools

import jax
import jax.numpy as jnp
from jax import lax
from jax.experimental import pallas as pl
from jax.experimental.pallas import tpu as pltpu
from jax.sharding import PartitionSpec as P

BF16, F32 = jnp.bfloat16, jnp.float32
LANES = 128


def pairwise(value, bit):
    count = lax.axis_size("seq")
    if bit == 0:
        pairs = [(i, i ^ 1) for i in range(count)]
    else:
        pairs = [(i, i + 1) for i in range(1, count - 1, 2)] + [(i + 1, i) for i in range(1, count - 1, 2)]
    return lax.ppermute(value, "seq", pairs)


def mirrored(value):
    return lax.ppermute(value, "strand", [(0, 1), (1, 0)])


def dot(a, b):
    return lax.dot_general(a, b, (((1,), (0,)), ((), ())), preferred_element_type=F32)


def dot_t(a, b):
    return lax.dot_general(a, b, (((1,), (1,)), ((), ())), preferred_element_type=F32)


def at(start, size):
    return pl.ds(pl.multiple_of(start, LANES), size)


def call(kernel, ins, outs, flops, scratch=(), limit=14, space=pltpu.VMEM):
    moved = sum(a.size * a.dtype.itemsize for a in ins) + sum(
        o.size * jnp.dtype(o.dtype).itemsize for o in outs
    )

    def body(*refs):
        kernel((lax.rem(lax.axis_index("seq"), 2), lax.axis_index("head")), *refs)

    return pl.pallas_call(
        body,
        out_shape=outs,
        in_specs=[pl.BlockSpec(memory_space=pltpu.VMEM)] * len(ins),
        out_specs=[pl.BlockSpec(memory_space=space)] * len(outs),
        scratch_shapes=list(scratch),
        compiler_params=pltpu.CompilerParams(vmem_limit_bytes=limit << 20),
        cost_estimate=pl.CostEstimate(flops=flops, bytes_accessed=moved, transcendentals=0),
    )(*ins)


def shape(dims, kind):
    return jax.ShapeDtypeStruct(dims, kind)


def split(place, taps, out, mix, sent):
    head = place[1]
    wide = sent.shape[3] - LANES
    carried = jnp.where(head == 3, out[...], taps[jnp.minimum(head, 2)])
    for c in range(2):
        column = (2 * jnp.minimum(head, 2) + c) * LANES
        sent[0, c, :, :wide] = carried[:, c * wide : (c + 1) * wide]
        sent[0, c, :, wide:] = mix[:, at(column, LANES)]
    for k in range(1, sent.shape[0]):
        sent[k] = sent[0]


def repack(lanes, place, line, sent):
    deep = line.shape[1]
    for z in range(sent.shape[1]):
        sent[0, z, :deep, :] = line[2 * z, :, lanes]
        sent[0, z, deep:, :] = line[2 * z + 1, :, lanes]
    for k in range(1, sent.shape[0]):
        sent[k] = sent[0]


def mirror_sum(core, perm, top, mirror, both):
    half = both.shape[2]
    hot = (lax.broadcasted_iota(jnp.int32, (half, half), 0) == perm[...]).astype(BF16)
    both[0] = (top[:, :half].astype(F32) + dot(mirror[...], hot)).astype(BF16)
    both[1] = top[:, half:]


def restore(core, paired, own, other, edge, inner):
    c = core[0]
    rows, half = edge.shape
    for k in range(half // (2 * LANES)):
        for place, pieces in ((c, own), (1 - c, other)):
            column = (2 * k + place) * LANES
            mixing = dot(paired[0], pieces[k])
            b = (paired[1, :, at(column, LANES)].astype(F32) - mixing).astype(BF16)

            @pl.when(c == 0)
            def _():
                edge[:, at(column, LANES)] = b[:rows]
                inner[:, at(column, LANES)] = b[rows:]

            @pl.when(c == 1)
            def _():
                edge[:, at(column, LANES)] = b[rows:]
                inner[:, at(column, LANES)] = b[:rows]


def turn(core, perm, grads, own, other, turned, base, mix):
    c, head = core[0], core[1]
    side = turned.shape[0]
    wide = side // 2
    hot = (lax.broadcasted_iota(jnp.int32, (side, side), 0) == perm[...]).astype(BF16)
    for place, pieces in ((c, own), (1 - c, other)):
        for k in range(side // (2 * LANES)):
            row = at((2 * k + place) * LANES, LANES)
            block = pieces[k]
            mix[row, :] = block.T
            turned[row, :] = dot(hot, block).astype(BF16).T
    backed = dot(grads[head ^ 2], mix[:wide, :]) + dot(grads[head ^ 3], mix[wide:, :])
    for k in range(2):
        lane = slice(k * wide, (k + 1) * wide)
        base[:, lane] = grads[head ^ k].astype(F32) + backed[:, lane]


def branch(core, beyond, edge, inner, across, own, other, hidden, slope, out):
    c = core[0]
    _, half = edge.shape
    before = jnp.concatenate([beyond[...], edge[...]], axis=0)
    here = jnp.concatenate([edge[...], inner[...]], axis=0)
    after = jnp.concatenate([inner[...], across[...]], axis=0)
    wide = half // 2
    root = 0.7978845608028654
    for place, taps in ((c, own), (1 - c, other)):
        lane = at(place * wide, wide)
        pre = (
            dot(before, taps[2 * c])
            + dot(here, taps[1])
            + dot(after, taps[2 - 2 * c])
        )
        squared = pre * pre
        bent = jnp.tanh(root * (pre + 0.044715 * (pre * squared)))
        share = 0.5 * (1.0 + bent)
        slope[:, lane] = share + pre * (0.5 * (1.0 - bent * bent)) * (
            root * (1.0 + 3.0 * 0.044715 * squared)
        )
        hidden[:, lane] = (pre * share).astype(BF16)
        out[lane, :] = taps[3].T


def emit(core, top, hidden, edge, inner, own, other, after, restored):
    c = core[0]
    rows, half = edge.shape
    wide = half // 2
    lines = (at(c * rows, rows), at((1 - c) * rows, rows))
    for place, pieces in ((c, own), (1 - c, other)):
        lane = at(place * wide, wide)
        made = dot(hidden[...], pieces[3])
        for k, line in enumerate(lines):
            restored[line, lane] = (
                top[line, lane].astype(F32) - made[k * rows : (k + 1) * rows]
            ).astype(BF16)
    restored[lines[0], half:] = edge[...]
    restored[lines[1], half:] = inner[...]


def pull(core, upper, lower, turned, base, slope, out, cot, edge, inner):
    c = core[0]
    rows = edge.shape[0]
    wide = upper.shape[2]
    odd = core[1] & 1
    first = jnp.concatenate([upper[odd], lower[odd]], axis=0)
    second = jnp.concatenate([upper[1 - odd], lower[1 - odd]], axis=0)
    rounded = (base[...] + dot(first, turned[:wide, :]) + dot(second, turned[wide:, :])).astype(BF16)
    cot[...] = rounded
    pulled = dot(rounded, out[...])

    @pl.when(c == 0)
    def _():
        edge[...] = (pulled[:rows] * slope[:rows, :]).astype(BF16)
        inner[...] = (pulled[rows:] * slope[rows:, :]).astype(BF16)

    @pl.when(c == 1)
    def _():
        edge[...] = (pulled[rows:] * slope[:rows, :]).astype(BF16)
        inner[...] = (pulled[:rows] * slope[rows:, :]).astype(BF16)


def gather(core, grads, beyond, edge, inner, own, other, result, rest, near):
    c = core[0]
    rows, half = edge.shape
    wide = half // 2
    head = core[1]
    total = jnp.zeros((2 * rows, half), F32)
    low = jnp.zeros((rows, half), F32)
    for place, taps in ((c, own), (1 - c, other)):
        lane = at(place * wide, wide)
        e, i = edge[:, lane], inner[:, lane]
        total += dot_t(jnp.concatenate([e, i], axis=0), taps[1])
        total += dot_t(jnp.concatenate([beyond[:, lane], e], axis=0), taps[2 - 2 * c])
        low += dot_t(i, taps[2 * c])
        near[lane, :] = taps[2 * c].T
    lines = (at(c * rows, rows), at((1 - c) * rows, rows))
    plain = [
        jnp.concatenate([grads[head ^ 2, line, :], grads[head ^ 3, line, :]], axis=1).astype(F32)
        for line in lines
    ]
    result[...] = (plain[0] + total[:rows] + low).astype(BF16)
    rest[...] = plain[1] + total[rows:]


def finish(core, across, near, cot, edge_b, rest, result):
    c = core[0]
    rows = edge_b.shape[0]
    half = cot.shape[1]
    result[:, :half] = cot[...]
    result[at(c * rows, rows), half:] = edge_b[...]
    result[at((1 - c) * rows, rows), half:] = (rest[...] + dot(across[...], near[...])).astype(BF16)


def shards(top, grad_heads, tap_weight_grid, out_w, mix_w, rc_perm):
    half = top.shape[3] // 2
    rows = top.shape[2] // 2
    heads = lax.axis_size("head")
    ranks = 4
    lines = lax.axis_size("seq") // (2 * ranks)
    head = lax.axis_index("head")
    top = top[0, 0]

    deep = out_w.shape[0]
    (sent,) = call(
        split,
        (tap_weight_grid, out_w, mix_w),
        (shape((lines, 2, deep, half // 2 + LANES), BF16),),
        0,
        limit=60,
    )
    along = [[(y * lines + z) * 2 + c for z in range(lines) for c in range(2)] for y in range(ranks)]
    line = lax.all_to_all(sent.reshape(2 * lines, *sent.shape[2:]), "seq", 0, 0, axis_index_groups=along, tiled=True)
    ao = mirrored(top[:, :half])
    blocks = [lax.dynamic_index_in_dim(grad_heads[:, 0], head ^ k, 0, False) for k in range(heads)]
    grads = [blocks[0]]
    for k in range(1, heads):
        grads.append(lax.ppermute(blocks[k], "head", [(i, i ^ k) for i in range(heads)]))
    grads = jnp.stack(grads)

    go = []
    for k in range(2):
        start = (2 - (head // 2) * 2, k * rows, 0)
        go.append(mirrored(lax.dynamic_slice(grads, start, (2, rows, half // 2))))
    plane = [
        [h * 2 * lines * ranks + (y * lines + z) * 2 + c for h in range(heads) for y in range(ranks)]
        for z in range(lines)
        for c in range(2)
    ]


    def planar(first, last):
        (sent,) = call(
            functools.partial(repack, slice(first, last)),
            (line,),
            (shape((heads * ranks, lines, 2 * deep, last - first), BF16),),
            0,
        )
        found = lax.all_to_all(sent, ("head", "seq"), 0, 0, axis_index_groups=plane, tiled=True)
        return found.reshape(heads, half, last - first)

    mine_mix = planar(half // 2, half // 2 + LANES)
    mine = planar(0, half // 2)
    theirs_mix = pairwise(mine_mix, 0)
    theirs = pairwise(mine, 0)

    unit = 2 * rows * half * half
    square, tall, chunk = (half, half), (2 * rows, half), (rows, half)
    perm = rc_perm[None, :]
    (paired,) = call(mirror_sum, (perm, top, ao), (shape((2, *tall), BF16),), 2 * unit)
    edge, inner = call(
        restore, (paired, mine_mix, theirs_mix), (shape(chunk, BF16), shape(chunk, BF16)), 2 * unit
    )
    beyond = pairwise(edge, 1)
    across = pairwise(inner, 0)
    turned, base = call(
        turn,
        (perm, grads, mine_mix, theirs_mix),
        (shape(square, BF16), shape(tall, F32)),
        6 * unit,
        scratch=(pltpu.VMEM(square, BF16),),
    )
    hidden, slope, out = call(
        branch,
        (beyond, edge, inner, across, mine, theirs),
        (shape(tall, BF16), shape(tall, F32), shape(square, BF16)),
        6 * unit,
    )
    cot, held_edge, held_inner = call(
        pull,
        (*go, turned, base, slope, out),
        (shape(tall, BF16), shape(chunk, BF16), shape(chunk, BF16)),
        4 * unit,
    )
    cot_beyond = pairwise(held_edge, 1)
    cot_across = pairwise(held_inner, 0)
    (restored,) = call(
        emit,
        (top, hidden, edge, inner, mine, theirs, held_inner),
        (shape(top.shape, BF16),),
        2 * unit,
    )
    edge_b, rest, near = call(
        gather,
        (grads, cot_beyond, held_edge, held_inner, mine, theirs),
        (shape(chunk, BF16), shape(chunk, F32), shape(square, BF16)),
        5 * unit,
    )
    (result,) = call(
        finish,
        (cot_across, near, cot, edge_b, rest),
        (shape(top.shape, BF16),),
        unit,
    )
    return restored[None, None], result[None, None]


def solution(mesh):
    placed = (
        P("head", "strand", "seq", None),
        P(None, "strand", "seq", "head"),
        P(None, "seq", None),
        P("seq", None),
        P("seq", None),
        P(),
    )
    return jax.shard_map(
        shards,
        mesh=mesh,
        in_specs=placed,
        out_specs=(P("head", "strand", "seq", None), P("head", "strand", "seq", None)),
        check_vma=False,
    )
```

```python
import functools

import jax
import jax.numpy as jnp
from jax import lax
from jax.experimental import pallas as pl
from jax.experimental.pallas import tpu as pltpu
from jax.sharding import PartitionSpec as P

BF16, F32 = jnp.bfloat16, jnp.float32
LANES = 128
LATE = 192


def pairwise(value, bit):
    count = lax.axis_size("seq")
    if bit == 0:
        pairs = [(i, i ^ 1) for i in range(count)]
    else:
        pairs = [(i, i + 1) for i in range(1, count - 1, 2)] + [(i + 1, i) for i in range(1, count - 1, 2)]
    return lax.ppermute(value, "seq", pairs)


def mirrored(value):
    return lax.ppermute(value, "strand", [(0, 1), (1, 0)])


def dot(a, b):
    return lax.dot_general(a, b, (((1,), (0,)), ((), ())), preferred_element_type=F32)


def dot_t(a, b):
    return lax.dot_general(a, b, (((1,), (1,)), ((), ())), preferred_element_type=F32)


def at(start, size):
    return pl.ds(pl.multiple_of(start, LANES), size)


def call(kernel, ins, outs, flops, scratch=(), limit=14, space=pltpu.VMEM):
    moved = sum(a.size * a.dtype.itemsize for a in ins) + sum(
        o.size * jnp.dtype(o.dtype).itemsize for o in outs
    )

    def body(*refs):
        kernel((lax.rem(lax.axis_index("seq"), 2), lax.axis_index("head")), *refs)

    return pl.pallas_call(
        body,
        out_shape=outs,
        in_specs=[pl.BlockSpec(memory_space=pltpu.VMEM)] * len(ins),
        out_specs=[pl.BlockSpec(memory_space=space)] * len(outs),
        scratch_shapes=list(scratch),
        compiler_params=pltpu.CompilerParams(vmem_limit_bytes=limit << 20),
        cost_estimate=pl.CostEstimate(flops=flops, bytes_accessed=moved, transcendentals=0),
    )(*ins)


def shape(dims, kind):
    return jax.ShapeDtypeStruct(dims, kind)


def split(place, taps, out, mix, sent):
    head = place[1]
    wide = sent.shape[3] - LANES
    carried = jnp.where(head == 3, out[...], taps[jnp.minimum(head, 2)])
    for c in range(2):
        column = (2 * jnp.minimum(head, 2) + c) * LANES
        sent[0, c, :, :wide] = carried[:, c * wide : (c + 1) * wide]
        sent[0, c, :, wide:] = mix[:, at(column, LANES)]
    for k in range(1, sent.shape[0]):
        sent[k] = sent[0]


def repack(lanes, place, line, sent):
    deep = line.shape[1]
    for z in range(sent.shape[1]):
        sent[0, z, :deep, :] = line[2 * z, :, lanes]
        sent[0, z, deep:, :] = line[2 * z + 1, :, lanes]
    for k in range(1, sent.shape[0]):
        sent[k] = sent[0]


def mirror_sum(core, perm, top, mirror, both):
    half = both.shape[2]
    hot = (lax.broadcasted_iota(jnp.int32, (half, half), 0) == perm[...]).astype(BF16)
    both[0] = (top[:, :half].astype(F32) + dot(mirror[...], hot)).astype(BF16)
    both[1] = top[:, half:]


def restore(core, paired, own, other, edge, inner):
    c = core[0]
    rows, half = edge.shape
    for k in range(half // (2 * LANES)):
        for place, pieces in ((c, own), (1 - c, other)):
            column = (2 * k + place) * LANES
            mixing = dot(paired[0], pieces[k])
            b = (paired[1, :, at(column, LANES)].astype(F32) - mixing).astype(BF16)

            @pl.when(c == 0)
            def _():
                edge[:, at(column, LANES)] = b[:rows]
                inner[:, at(column, LANES)] = b[rows:]

            @pl.when(c == 1)
            def _():
                edge[:, at(column, LANES)] = b[rows:]
                inner[:, at(column, LANES)] = b[:rows]


def turn(core, perm, grads, own, other, turned, base, mix):
    c, head = core[0], core[1]
    side = turned.shape[0]
    wide = side // 2
    hot = (lax.broadcasted_iota(jnp.int32, (side, side), 0) == perm[...]).astype(BF16)
    for place, pieces in ((c, own), (1 - c, other)):
        for k in range(side // (2 * LANES)):
            row = at((2 * k + place) * LANES, LANES)
            block = pieces[k]
            mix[row, :] = block.T
            turned[row, :] = dot(hot, block).astype(BF16).T
    backed = dot(grads[head ^ 2], mix[:wide, :]) + dot(grads[head ^ 3], mix[wide:, :])
    for k in range(2):
        lane = slice(k * wide, (k + 1) * wide)
        base[:, lane] = grads[head ^ k].astype(F32) + backed[:, lane]


def branch(core, beyond, edge, inner, across, own, other, hidden, slope, out):
    c = core[0]
    _, half = edge.shape
    before = jnp.concatenate([beyond[...], edge[...]], axis=0)
    here = jnp.concatenate([edge[...], inner[...]], axis=0)
    after = jnp.concatenate([inner[...], across[...]], axis=0)
    wide = half // 2
    root = 0.7978845608028654
    for place, taps in ((c, own), (1 - c, other)):
        lane = at(place * wide, wide)
        pre = (
            dot(before, taps[2 * c])
            + dot(here, taps[1])
            + dot(after, taps[2 - 2 * c])
        )
        squared = pre * pre
        bent = jnp.tanh(root * (pre + 0.044715 * (pre * squared)))
        share = 0.5 * (1.0 + bent)
        slope[:, lane] = share + pre * (0.5 * (1.0 - bent * bent)) * (
            root * (1.0 + 3.0 * 0.044715 * squared)
        )
        hidden[:, lane] = (pre * share).astype(BF16)
        out[lane, :] = taps[3].T


def emit(core, top, hidden, edge, inner, own, other, after, restored):
    c = core[0]
    rows, half = edge.shape
    wide = half // 2
    lines = (at(c * rows, rows), at((1 - c) * rows, rows))
    for place, pieces in ((c, own), (1 - c, other)):
        lane = at(place * wide, wide)
        made = dot(hidden[...], pieces[3])
        for k, line in enumerate(lines):
            restored[line, lane] = (
                top[line, lane].astype(F32) - made[k * rows : (k + 1) * rows]
            ).astype(BF16)
    restored[lines[0], half:] = edge[...]
    restored[lines[1], half:] = inner[...]


def pull(core, upper, lower, turned, base, slope, out, cot, edge, inner):
    c = core[0]
    rows = edge.shape[0]
    wide = upper.shape[2]
    odd = core[1] & 1
    first = jnp.concatenate([upper[odd], lower[odd]], axis=0)
    second = jnp.concatenate([upper[1 - odd], lower[1 - odd]], axis=0)
    rounded = (base[...] + dot(first, turned[:wide, :]) + dot(second, turned[wide:, :])).astype(BF16)
    cot[...] = rounded
    pulled = dot(rounded, out[...])

    @pl.when(c == 0)
    def _():
        edge[...] = (pulled[:rows] * slope[:rows, :]).astype(BF16)
        inner[...] = (pulled[rows:] * slope[rows:, :]).astype(BF16)

    @pl.when(c == 1)
    def _():
        edge[...] = (pulled[rows:] * slope[:rows, :]).astype(BF16)
        inner[...] = (pulled[:rows] * slope[rows:, :]).astype(BF16)


def gather(core, grads, edge, inner, own, other, edge_rest, inner_rest, near, far):
    c = core[0]
    rows, half = edge.shape
    wide = half // 2
    total = jnp.zeros((2 * rows, half), F32)
    low = jnp.zeros((rows, half), F32)
    high = jnp.zeros((rows, half), F32)
    for place, taps in ((c, own), (1 - c, other)):
        lane = at(place * wide, wide)
        e, i = edge[:, lane], inner[:, lane]
        total += dot_t(jnp.concatenate([e, i], axis=0), taps[1])
        low += dot_t(i, taps[2 * c])
        high += dot_t(e, taps[2 - 2 * c])
        near[lane, :] = taps[2 * c].T
        far[lane, :] = taps[2 - 2 * c].T
    first, second = (
        jnp.concatenate([grads[core[1] ^ 2, line, :], grads[core[1] ^ 3, line, :]], axis=1).astype(F32)
        for line in (at(c * rows, rows), at((1 - c) * rows, rows))
    )
    edge_rest[...] = first + total[:rows] + low
    inner_rest[...] = second + total[rows:] + high


def finish(core, across, beyond, near, far, cot, edge_rest, inner_rest, result):
    c = core[0]
    rows, half = edge_rest.shape
    result[:, :half] = cot[...]
    result[at(c * rows, rows), half:] = (edge_rest[...] + dot(beyond[...], far[...])).astype(BF16)
    result[at((1 - c) * rows, rows), half:] = (inner_rest[...] + dot(across[...], near[...])).astype(BF16)


def shards(top, grad_heads, tap_weight_grid, out_w, mix_w, rc_perm):
    half = top.shape[3] // 2
    rows = top.shape[2] // 2
    heads = lax.axis_size("head")
    ranks = 4
    lines = lax.axis_size("seq") // (2 * ranks)
    head = lax.axis_index("head")
    top = top[0, 0]

    deep = out_w.shape[0]
    (sent,) = call(
        split,
        (tap_weight_grid, out_w, mix_w),
        (shape((lines, 2, deep, half // 2 + LANES), BF16),),
        0,
        limit=60,
    )
    along = [[(y * lines + z) * 2 + c for z in range(lines) for c in range(2)] for y in range(ranks)]
    line = lax.all_to_all(sent.reshape(2 * lines, *sent.shape[2:]), "seq", 0, 0, axis_index_groups=along, tiled=True)
    ao = mirrored(top[:, :half])
    blocks = [lax.dynamic_index_in_dim(grad_heads[:, 0], head ^ k, 0, False) for k in range(heads)]
    grads = [blocks[0]]
    for k in range(1, heads):
        grads.append(lax.ppermute(blocks[k], "head", [(i, i ^ k) for i in range(heads)]))
    grads = jnp.stack(grads)

    go = []
    for first, count in ((0, 2 * rows - LATE), (2 * rows - LATE, LATE)):
        start = (2 - (head // 2) * 2, first, 0)
        go.append(mirrored(lax.dynamic_slice(grads, start, (2, count, half // 2))))
    plane = [
        [h * 2 * lines * ranks + (y * lines + z) * 2 + c for h in range(heads) for y in range(ranks)]
        for z in range(lines)
        for c in range(2)
    ]


    def planar(first, last):
        (sent,) = call(
            functools.partial(repack, slice(first, last)),
            (line,),
            (shape((heads * ranks, lines, 2 * deep, last - first), BF16),),
            0,
        )
        found = lax.all_to_all(sent, ("head", "seq"), 0, 0, axis_index_groups=plane, tiled=True)
        return found.reshape(heads, half, last - first)

    mine_mix = planar(half // 2, half // 2 + LANES)
    mine = planar(0, half // 2)
    theirs_mix = pairwise(mine_mix, 0)
    theirs = pairwise(mine, 0)

    unit = 2 * rows * half * half
    square, tall, chunk = (half, half), (2 * rows, half), (rows, half)
    perm = rc_perm[None, :]
    (paired,) = call(mirror_sum, (perm, top, ao), (shape((2, *tall), BF16),), 2 * unit)
    edge, inner = call(
        restore, (paired, mine_mix, theirs_mix), (shape(chunk, BF16), shape(chunk, BF16)), 2 * unit
    )
    beyond = pairwise(edge, 1)
    across = pairwise(inner, 0)
    turned, base = call(
        turn,
        (perm, grads, mine_mix, theirs_mix),
        (shape(square, BF16), shape(tall, F32)),
        6 * unit,
        scratch=(pltpu.VMEM(square, BF16),),
    )
    hidden, slope, out = call(
        branch,
        (beyond, edge, inner, across, mine, theirs),
        (shape(tall, BF16), shape(tall, F32), shape(square, BF16)),
        6 * unit,
    )
    cot, held_edge, held_inner = call(
        pull,
        (*go, turned, base, slope, out),
        (shape(tall, BF16), shape(chunk, BF16), shape(chunk, BF16)),
        4 * unit,
    )
    cot_beyond = pairwise(held_edge, 1)
    cot_across = pairwise(held_inner, 0)
    (restored,) = call(
        emit,
        (top, hidden, edge, inner, mine, theirs, held_inner),
        (shape(top.shape, BF16),),
        2 * unit,
    )
    edge_rest, inner_rest, near, far = call(
        gather,
        (grads, held_edge, held_inner, mine, theirs),
        (shape(chunk, F32), shape(chunk, F32), shape(square, BF16), shape(square, BF16)),
        4 * unit,
    )
    (result,) = call(
        finish,
        (cot_across, cot_beyond, near, far, cot, edge_rest, inner_rest),
        (shape(top.shape, BF16),),
        2 * unit,
    )
    return restored[None, None], result[None, None]


def solution(mesh):
    placed = (
        P("head", "strand", "seq", None),
        P(None, "strand", "seq", "head"),
        P(None, "seq", None),
        P("seq", None),
        P("seq", None),
        P(),
    )
    return jax.shard_map(
        shards,
        mesh=mesh,
        in_specs=placed,
        out_specs=(P("head", "strand", "seq", None), P("head", "strand", "seq", None)),
        check_vma=False,
    )
```

```python
import functools

import jax
import jax.numpy as jnp
from jax import lax
from jax.experimental import pallas as pl
from jax.experimental.pallas import tpu as pltpu
from jax.sharding import PartitionSpec as P

BF16, F32 = jnp.bfloat16, jnp.float32
LANES = 128
LATE = 192


def pairwise(value, bit):
    count = lax.axis_size("seq")
    if bit == 0:
        pairs = [(i, i ^ 1) for i in range(count)]
    else:
        pairs = [(i, i + 1) for i in range(1, count - 1, 2)] + [(i + 1, i) for i in range(1, count - 1, 2)]
    return lax.ppermute(value, "seq", pairs)


def mirrored(value):
    return lax.ppermute(value, "strand", [(0, 1), (1, 0)])


def dot(a, b):
    return lax.dot_general(a, b, (((1,), (0,)), ((), ())), preferred_element_type=F32)


def dot_t(a, b):
    return lax.dot_general(a, b, (((1,), (1,)), ((), ())), preferred_element_type=F32)


def at(start, size):
    return pl.ds(pl.multiple_of(start, LANES), size)


def call(kernel, ins, outs, flops, scratch=(), limit=14, space=pltpu.VMEM):
    moved = sum(a.size * a.dtype.itemsize for a in ins) + sum(
        o.size * jnp.dtype(o.dtype).itemsize for o in outs
    )

    def body(*refs):
        kernel((lax.rem(lax.axis_index("seq"), 2), lax.axis_index("head")), *refs)

    return pl.pallas_call(
        body,
        out_shape=outs,
        in_specs=[pl.BlockSpec(memory_space=pltpu.VMEM)] * len(ins),
        out_specs=[pl.BlockSpec(memory_space=space)] * len(outs),
        scratch_shapes=list(scratch),
        compiler_params=pltpu.CompilerParams(vmem_limit_bytes=limit << 20),
        cost_estimate=pl.CostEstimate(flops=flops, bytes_accessed=moved, transcendentals=0),
    )(*ins)


def shape(dims, kind):
    return jax.ShapeDtypeStruct(dims, kind)


def split(place, taps, out, mix, sent):
    head = place[1]
    wide = sent.shape[3] - LANES
    carried = jnp.where(head == 3, out[...], taps[jnp.minimum(head, 2)])
    for c in range(2):
        column = (2 * jnp.minimum(head, 2) + c) * LANES
        sent[0, c, :, :wide] = carried[:, c * wide : (c + 1) * wide]
        sent[0, c, :, wide:] = mix[:, at(column, LANES)]
    for k in range(1, sent.shape[0]):
        sent[k] = sent[0]


def repack(lanes, place, line, sent):
    deep = line.shape[1]
    for z in range(sent.shape[1]):
        sent[0, z, :deep, :] = line[2 * z, :, lanes]
        sent[0, z, deep:, :] = line[2 * z + 1, :, lanes]
    for k in range(1, sent.shape[0]):
        sent[k] = sent[0]


def mirror_sum(core, perm, top, mirror, paired):
    half = paired.shape[1]
    hot = (lax.broadcasted_iota(jnp.int32, (half, half), 0) == perm[...]).astype(BF16)
    paired[...] = (top[:, :half].astype(F32) + dot(mirror[...], hot)).astype(BF16)


def restore(core, top, paired, own, other, edge, inner):
    c = core[0]
    rows, half = edge.shape
    for k in range(half // (2 * LANES)):
        for place, pieces in ((c, own), (1 - c, other)):
            column = (2 * k + place) * LANES
            mixing = dot(paired[...], pieces[k])
            b = (top[:, at(half + column, LANES)].astype(F32) - mixing).astype(BF16)

            @pl.when(c == 0)
            def _():
                edge[:, at(column, LANES)] = b[:rows]
                inner[:, at(column, LANES)] = b[rows:]

            @pl.when(c == 1)
            def _():
                edge[:, at(column, LANES)] = b[rows:]
                inner[:, at(column, LANES)] = b[:rows]


def turn(core, perm, grads, own, other, turned, base, mix):
    c, head = core[0], core[1]
    side = turned.shape[0]
    wide = side // 2
    hot = (lax.broadcasted_iota(jnp.int32, (side, side), 0) == perm[...]).astype(BF16)
    for place, pieces in ((c, own), (1 - c, other)):
        for k in range(side // (2 * LANES)):
            row = at((2 * k + place) * LANES, LANES)
            block = pieces[k]
            mix[row, :] = block.T
            turned[row, :] = dot(hot, block).astype(BF16).T
    backed = dot(grads[head ^ 2], mix[:wide, :]) + dot(grads[head ^ 3], mix[wide:, :])
    for k in range(2):
        lane = slice(k * wide, (k + 1) * wide)
        base[:, lane] = grads[head ^ k].astype(F32) + backed[:, lane]


def branch(core, beyond, edge, inner, across, own, other, hidden, slope, out):
    c = core[0]
    _, half = edge.shape
    before = jnp.concatenate([beyond[...], edge[...]], axis=0)
    here = jnp.concatenate([edge[...], inner[...]], axis=0)
    after = jnp.concatenate([inner[...], across[...]], axis=0)
    wide = half // 2
    root = 0.7978845608028654
    for place, taps in ((c, own), (1 - c, other)):
        lane = at(place * wide, wide)
        pre = (
            dot(before, taps[2 * c])
            + dot(here, taps[1])
            + dot(after, taps[2 - 2 * c])
        )
        squared = pre * pre
        bent = jnp.tanh(root * (pre + 0.044715 * (pre * squared)))
        share = 0.5 * (1.0 + bent)
        slope[:, lane] = share + pre * (0.5 * (1.0 - bent * bent)) * (
            root * (1.0 + 3.0 * 0.044715 * squared)
        )
        hidden[:, lane] = (pre * share).astype(BF16)
        out[lane, :] = taps[3].T


def emit(core, top, hidden, edge, inner, own, other, after, restored):
    c = core[0]
    rows, half = edge.shape
    wide = half // 2
    lines = (at(c * rows, rows), at((1 - c) * rows, rows))
    for place, pieces in ((c, own), (1 - c, other)):
        lane = at(place * wide, wide)
        made = dot(hidden[...], pieces[3])
        for k, line in enumerate(lines):
            restored[line, lane] = (
                top[line, lane].astype(F32) - made[k * rows : (k + 1) * rows]
            ).astype(BF16)
    restored[lines[0], half:] = edge[...]
    restored[lines[1], half:] = inner[...]


def pull(core, upper, lower, turned, base, slope, out, cot, edge, inner):
    c = core[0]
    rows = edge.shape[0]
    wide = upper.shape[2]
    odd = core[1] & 1
    first = jnp.concatenate([upper[odd], lower[odd]], axis=0)
    second = jnp.concatenate([upper[1 - odd], lower[1 - odd]], axis=0)
    rounded = (base[...] + dot(first, turned[:wide, :]) + dot(second, turned[wide:, :])).astype(BF16)
    cot[...] = rounded
    pulled = dot(rounded, out[...])

    @pl.when(c == 0)
    def _():
        edge[...] = (pulled[:rows] * slope[:rows, :]).astype(BF16)
        inner[...] = (pulled[rows:] * slope[rows:, :]).astype(BF16)

    @pl.when(c == 1)
    def _():
        edge[...] = (pulled[rows:] * slope[:rows, :]).astype(BF16)
        inner[...] = (pulled[:rows] * slope[rows:, :]).astype(BF16)


def gather(core, grads, edge, inner, own, other, edge_rest, inner_rest, near, far):
    c = core[0]
    rows, half = edge.shape
    wide = half // 2
    total = jnp.zeros((2 * rows, half), F32)
    low = jnp.zeros((rows, half), F32)
    high = jnp.zeros((rows, half), F32)
    for place, taps in ((c, own), (1 - c, other)):
        lane = at(place * wide, wide)
        e, i = edge[:, lane], inner[:, lane]
        total += dot_t(jnp.concatenate([e, i], axis=0), taps[1])
        low += dot_t(i, taps[2 * c])
        high += dot_t(e, taps[2 - 2 * c])
        near[lane, :] = taps[2 * c].T
        far[lane, :] = taps[2 - 2 * c].T
    first, second = (
        jnp.concatenate([grads[core[1] ^ 2, line, :], grads[core[1] ^ 3, line, :]], axis=1).astype(F32)
        for line in (at(c * rows, rows), at((1 - c) * rows, rows))
    )
    edge_rest[...] = first + total[:rows] + low
    inner_rest[...] = second + total[rows:] + high


def finish(core, across, beyond, near, far, cot, edge_rest, inner_rest, result):
    c = core[0]
    rows, half = edge_rest.shape
    result[:, :half] = cot[...]
    result[at(c * rows, rows), half:] = (edge_rest[...] + dot(beyond[...], far[...])).astype(BF16)
    result[at((1 - c) * rows, rows), half:] = (inner_rest[...] + dot(across[...], near[...])).astype(BF16)


def shards(top, grad_heads, tap_weight_grid, out_w, mix_w, rc_perm):
    half = top.shape[3] // 2
    rows = top.shape[2] // 2
    heads = lax.axis_size("head")
    ranks = 4
    lines = lax.axis_size("seq") // (2 * ranks)
    head = lax.axis_index("head")
    top = top[0, 0]

    deep = out_w.shape[0]
    (sent,) = call(
        split,
        (tap_weight_grid, out_w, mix_w),
        (shape((lines, 2, deep, half // 2 + LANES), BF16),),
        0,
        limit=60,
    )
    along = [[(y * lines + z) * 2 + c for z in range(lines) for c in range(2)] for y in range(ranks)]
    line = lax.all_to_all(sent.reshape(2 * lines, *sent.shape[2:]), "seq", 0, 0, axis_index_groups=along, tiled=True)
    ao = mirrored(top[:, :half])
    blocks = [lax.dynamic_index_in_dim(grad_heads[:, 0], head ^ k, 0, False) for k in range(heads)]
    grads = [blocks[0]]
    for k in range(1, heads):
        grads.append(lax.ppermute(blocks[k], "head", [(i, i ^ k) for i in range(heads)]))
    grads = jnp.stack(grads)

    go = []
    for first, count in ((0, 2 * rows - LATE), (2 * rows - LATE, LATE)):
        start = (2 - (head // 2) * 2, first, 0)
        go.append(mirrored(lax.dynamic_slice(grads, start, (2, count, half // 2))))
    plane = [
        [h * 2 * lines * ranks + (y * lines + z) * 2 + c for h in range(heads) for y in range(ranks)]
        for z in range(lines)
        for c in range(2)
    ]


    def planar(first, last):
        (sent,) = call(
            functools.partial(repack, slice(first, last)),
            (line,),
            (shape((heads * ranks, lines, 2 * deep, last - first), BF16),),
            0,
        )
        found = lax.all_to_all(sent, ("head", "seq"), 0, 0, axis_index_groups=plane, tiled=True)
        return found.reshape(heads, half, last - first)

    mine_mix = planar(half // 2, half // 2 + LANES)
    mine = planar(0, half // 2)
    theirs_mix = pairwise(mine_mix, 0)
    theirs = pairwise(mine, 0)

    unit = 2 * rows * half * half
    square, tall, chunk = (half, half), (2 * rows, half), (rows, half)
    perm = rc_perm[None, :]
    (paired,) = call(mirror_sum, (perm, top, ao), (shape(tall, BF16),), 2 * unit)
    edge, inner = call(
        restore, (top, paired, mine_mix, theirs_mix), (shape(chunk, BF16), shape(chunk, BF16)), 2 * unit
    )
    beyond = pairwise(edge, 1)
    across = pairwise(inner, 0)
    turned, base = call(
        turn,
        (perm, grads, mine_mix, theirs_mix),
        (shape(square, BF16), shape(tall, F32)),
        6 * unit,
        scratch=(pltpu.VMEM(square, BF16),),
    )
    hidden, slope, out = call(
        branch,
        (beyond, edge, inner, across, mine, theirs),
        (shape(tall, BF16), shape(tall, F32), shape(square, BF16)),
        6 * unit,
    )
    cot, held_edge, held_inner = call(
        pull,
        (*go, turned, base, slope, out),
        (shape(tall, BF16), shape(chunk, BF16), shape(chunk, BF16)),
        4 * unit,
    )
    cot_beyond = pairwise(held_edge, 1)
    cot_across = pairwise(held_inner, 0)
    (restored,) = call(
        emit,
        (top, hidden, edge, inner, mine, theirs, held_inner),
        (shape(top.shape, BF16),),
        2 * unit,
    )
    edge_rest, inner_rest, near, far = call(
        gather,
        (grads, held_edge, held_inner, mine, theirs),
        (shape(chunk, F32), shape(chunk, F32), shape(square, BF16), shape(square, BF16)),
        4 * unit,
    )
    (result,) = call(
        finish,
        (cot_across, cot_beyond, near, far, cot, edge_rest, inner_rest),
        (shape(top.shape, BF16),),
        2 * unit,
    )
    return restored[None, None], result[None, None]


def solution(mesh):
    placed = (
        P("head", "strand", "seq", None),
        P(None, "strand", "seq", "head"),
        P(None, "seq", None),
        P("seq", None),
        P("seq", None),
        P(),
    )
    return jax.shard_map(
        shards,
        mesh=mesh,
        in_specs=placed,
        out_specs=(P("head", "strand", "seq", None), P("head", "strand", "seq", None)),
        check_vma=False,
    )
```
